512 devices in a mesh: pipe: 32 (over z, y_hi, core), expert: 16 (over x, y_lo).
Axes of the slice: x: 4, y: 8 (y_hi: 2, y_lo: 4; y = y_hi * 4 + y_lo), z: 8, core: 2. Of those that a mesh axis runs over, the one named last changes fastest.
Arguments:
- fwd_in: bfloat16 [32, 1024, 3584], P('pipe', 'expert'), may hold values from -6 to 6
- bwd_in: bfloat16 [32, 1024, 3584], P('pipe', 'expert'), may hold values from -6 to 6
- bwd_grad_in: bfloat16 [32, 1024, 3584], P('pipe', 'expert'), may hold values from -6 to 6
- w_gate: bfloat16 [32, 7168, 1024], P('pipe', 'expert'), may hold values from -0.09375 to 0.09375
- w_up: bfloat16 [32, 7168, 1024], P('pipe', 'expert'), may hold values from -0.09375 to 0.09375
- w_down: bfloat16 [32, 1024, 7168], P('pipe', None, 'expert'), may hold values from -0.1875 to 0.1875
- fwd_ids: int32 [32, 1024, 1], P('pipe', 'expert'), may hold values from 0 to 1; in each aligned block of 64 rows (0 to 63, 64 to 127, ..., all dimensions but the last counted through in order) at most 40 rows name the same one
- fwd_gates: float32 [32, 1024, 1], P('pipe', 'expert'), may hold values from 0.25 to 1
- bwd_ids: int32 [32, 1024, 1], P('pipe', 'expert'), may hold values from 0 to 1; in each aligned block of 64 rows (0 to 63, 64 to 127, ..., all dimensions but the last counted through in order) at most 40 rows name the same one
- bwd_gates: float32 [32, 1024, 1], P('pipe', 'expert'), may hold values from 0.25 to 1
Outputs:
- fwd_out: bfloat16 [32, 1024, 3584], P('pipe', 'expert')
- bwd_out: bfloat16 [32, 1024, 3584], P('pipe', 'expert')
The draws below stay inside these ranges and needn't reach their ends.
Inputs may be any that keep to these rules, and one draw needn't show every extreme that they name: `fwd_ids`: each row names 1 different experts; among the 64 tokens of one device (aligned blocks of rows) no expert is named more than 40 times. `bwd_ids`: each row names 1 different experts; among the 64 tokens of one device (aligned blocks of rows) no expert is named more than 40 times.
All inputs are finite; a program needn't handle non-finite values.
Results may differ from the reference program's by a relative error of at most 0.01.
Values may be sent and summed in bfloat16 or wider, within the bound.
A program may use at most 128 MiB of HBM per device.

```python
import math
import jax
import jax.numpy as jnp
import numpy as np
from jax import lax

D = 3584
FF = 1024
EXPERTS = 2
TOP = 1
TOK_DEV = 64
CAP = 40
GROUP = 8
SECTIONS = 32
TOKENS = 1024


def shard_levels(own_key, dims, split, least, largest):
    level = 1.0
    for position, blocks in split:
        draws = jax.random.uniform(jax.random.fold_in(jax.random.fold_in(own_key, 6), position), (blocks,), jnp.float32, least / len(split), largest / len(split))
        level = level * jnp.repeat(jnp.exp(draws), dims[position] // blocks).reshape((-1,) + (1,) * (len(dims) - 1 - position))
    return level


def assign_block(rng, own, number, rows, number_of, top, most, skew):
    order = jax.random.permutation(rng, number_of)
    crowded, usual = portions_of(number_of, rows * top, most, skew, True), portions_of(number_of, rows * top, most, skew, False)
    places = jnp.arange(number_of)

    def named(tallies, offset_by):
        used = int((tallies > 0).sum())
        fixed = max(1, used // 4)
        passed = fixed + (places - fixed + offset_by * (used - fixed)) % max(1, number_of - fixed)
        return jnp.zeros((number_of,), jnp.int32).at[order[jnp.where(places < fixed, places, passed)]].set(jnp.asarray(tallies, jnp.int32))

    tallies = jnp.where(number % 4 == 0, named(crowded, number // 4), named(usual, number - number // 4 - 1))
    mixed = jax.random.permutation(jax.random.fold_in(own, 3), number_of)
    source_of, receiver = mixed[0:number_of // 2 * 2:2], mixed[1:number_of // 2 * 2:2]
    margin = jnp.minimum(tallies[source_of] - 1, most - tallies[receiver]) // 2
    margin = jnp.where((source_of == order[0]) | (receiver == order[0]) | (tallies[receiver] == 0), 0, jnp.maximum(margin, 0))
    passed = jax.random.randint(jax.random.fold_in(own, 4), (number_of // 2,), 0, 1 << 20) % (margin + 1)
    tallies = tallies.at[source_of].add(-passed).at[receiver].add(passed)
    members = jnp.searchsorted(jnp.cumsum(tallies), jnp.arange(rows * top), side="right").astype(jnp.int32)
    grid = members.reshape(top, rows).T
    grid = grid[jax.random.permutation(jax.random.fold_in(own, 1), rows)]
    offset_by = jax.random.randint(jax.random.fold_in(own, 2), (rows, 1), 0, top)
    return jnp.take_along_axis(grid, (jnp.arange(top)[None, :] + offset_by) % top, axis=1)


def portions_of(count, total, most, skew, full):
    loads = [(1 << 20) // math.isqrt(grade ** skew) + 1 for grade in range(1, count + 1)]
    largest = most if full else min(most, max(-(-total // count), total * loads[0] // sum(loads)))
    least = 1 if total - largest >= count - 1 else 0
    holding, surplus = [largest] + [least] * (count - 1), total - largest - least * (count - 1)
    while surplus > 0:
        candidates = [i for i in range(1, count) if holding[i] < largest] or [i for i in range(1, count) if holding[i] < most]
        mass, remaining = sum([loads[i] for i in candidates]), surplus
        for i in candidates:
            addition = min(most - holding[i], max(1, remaining * loads[i] // mass), surplus)
            holding[i] = holding[i] + addition
            surplus = surplus - addition
    return np.array(holding)


def noise(stream_key, extent, scale, limit, shards=(), kind=jnp.bfloat16):
    result = scale * jax.random.normal(stream_key, extent, jnp.float32)
    if shards:
        result = result * shard_levels(stream_key, extent, shards, -0.22, 0.18)
    return jnp.clip(result, -limit, limit).astype(kind)


def setup_inputs(seed: int = 0) -> dict:
    key_list = jax.random.split(jax.random.key(seed), 11)
    fwd_in = noise(key_list[0], (SECTIONS, TOKENS, D), 1.0, 6.0, ((0, 32), (1, 16)))
    bwd_in = noise(key_list[1], (SECTIONS, TOKENS, D), 1.0, 6.0, ((0, 32), (1, 16)))
    bwd_grad_in = noise(key_list[2], (SECTIONS, TOKENS, D), 1.0, 6.0, ((0, 32), (1, 16)))
    w_gate = noise(key_list[3], (SECTIONS, EXPERTS * D, FF), D ** -0.5, 0.09375, ((0, 32), (1, 16)))
    w_up = noise(key_list[4], (SECTIONS, EXPERTS * D, FF), D ** -0.5, 0.09375, ((0, 32), (1, 16)))
    w_down = noise(key_list[5], (SECTIONS, FF, EXPERTS * D), FF ** -0.5, 0.1875, ((0, 32), (2, 16)))
    fwd_ids_keys = jax.random.split(jax.random.fold_in(key_list[6], 1), SECTIONS * TOKENS // TOK_DEV)
    fwd_ids_turns = jax.random.permutation(jax.random.fold_in(key_list[6], 3), SECTIONS * TOKENS // TOK_DEV)
    fwd_ids = jax.vmap(lambda own, number: assign_block(jax.random.fold_in(key_list[6], 2), own, number, TOK_DEV, EXPERTS, TOP, CAP, 1))(fwd_ids_keys, fwd_ids_turns).reshape((SECTIONS, TOKENS, TOP))
    fwd_gates = jnp.clip(0.25 + 0.75 * jax.random.uniform(key_list[7], (SECTIONS, TOKENS, TOP), jnp.float32) ** shard_levels(key_list[7], (SECTIONS, TOKENS, TOP), ((0, 32), (1, 16)), -0.2, 0.2), 0.25, 1.0)
    bwd_ids_keys = jax.random.split(jax.random.fold_in(key_list[8], 1), SECTIONS * TOKENS // TOK_DEV)
    bwd_ids_turns = jax.random.permutation(jax.random.fold_in(key_list[8], 3), SECTIONS * TOKENS // TOK_DEV)
    bwd_ids = jax.vmap(lambda own, number: assign_block(jax.random.fold_in(key_list[8], 2), own, number, TOK_DEV, EXPERTS, TOP, CAP, 1))(bwd_ids_keys, bwd_ids_turns).reshape((SECTIONS, TOKENS, TOP))
    bwd_gates = jnp.clip(0.25 + 0.75 * jax.random.uniform(key_list[9], (SECTIONS, TOKENS, TOP), jnp.float32) ** shard_levels(key_list[9], (SECTIONS, TOKENS, TOP), ((0, 32), (1, 16)), -0.2, 0.2), 0.25, 1.0)
    return {"fwd_in": fwd_in, "bwd_in": bwd_in, "bwd_grad_in": bwd_grad_in, "w_gate": w_gate, "w_up": w_up, "w_down": w_down, "fwd_ids": fwd_ids, "fwd_gates": fwd_gates, "bwd_ids": bwd_ids, "bwd_gates": bwd_gates}


def slice_sum(rows, mats):
    token_count = rows.shape[0]
    width = rows.shape[1] // GROUP
    pieces = rows.reshape(token_count, GROUP, width).astype(jnp.float32)
    blocks = mats.reshape(GROUP, width, mats.shape[1]).astype(jnp.float32)
    partial_value = jnp.einsum("tgk,gkc->gtc", pieces, blocks).astype(jnp.bfloat16)
    return jnp.sum(partial_value.astype(jnp.float32), axis=0)


def forward_section(inputs, expert_ids, gate_values, gate_all, up_all, down_all):
    def one_expert(total, expert):
        joined = jnp.concatenate([gate_all[expert], up_all[expert]], axis=1)
        summed = slice_sum(inputs, joined)
        hidden = (jax.nn.silu(summed[:, :FF]) * summed[:, FF:]).astype(jnp.bfloat16)
        expert_out = jnp.dot(hidden, down_all[expert], preferred_element_type=jnp.float32).astype(jnp.bfloat16)
        weight = jnp.sum(jnp.where(expert_ids == expert, gate_values, 0.0), axis=1)
        return total + weight[:, None] * expert_out.astype(jnp.float32), None

    start = jnp.zeros(inputs.shape, jnp.float32)
    total, unused = lax.scan(one_expert, start, jnp.arange(EXPERTS, dtype=jnp.int32))
    return (inputs.astype(jnp.float32) + total).astype(jnp.bfloat16)


def backward_section(inputs, grads, expert_ids, gate_values, gate_all, up_all, down_all):
    def one_expert(total, expert):
        gate_mat = gate_all[expert]
        up_mat = up_all[expert]
        joined = jnp.concatenate([gate_mat, up_mat], axis=1)
        summed = slice_sum(inputs, joined)
        back_gate = summed[:, :FF]
        back_up = summed[:, FF:]
        grad_hidden = slice_sum(grads, down_all[expert].T)
        sig_gate = jax.nn.sigmoid(back_gate)
        grad_gate = (grad_hidden * back_up * sig_gate * (1.0 + back_gate * (1.0 - sig_gate))).astype(jnp.bfloat16)
        grad_up = (grad_hidden * jax.nn.silu(back_gate)).astype(jnp.bfloat16)
        expert_grad = jnp.dot(grad_gate, gate_mat.T, preferred_element_type=jnp.float32)
        expert_grad = expert_grad + jnp.dot(grad_up, up_mat.T, preferred_element_type=jnp.float32)
        expert_grad = expert_grad.astype(jnp.bfloat16)
        weight = jnp.sum(jnp.where(expert_ids == expert, gate_values, 0.0), axis=1)
        return total + weight[:, None] * expert_grad.astype(jnp.float32), None

    start = jnp.zeros(inputs.shape, jnp.float32)
    total, unused = lax.scan(one_expert, start, jnp.arange(EXPERTS, dtype=jnp.int32))
    return (grads.astype(jnp.float32) + total).astype(jnp.bfloat16)


def reference(fwd_in, bwd_in, bwd_grad_in, w_gate, w_up, w_down, fwd_ids, fwd_gates, bwd_ids, bwd_gates):
    section_x = jnp.concatenate([fwd_in[:1], fwd_in[:-1]], axis=0)
    section_g = jnp.concatenate([bwd_grad_in[1:], bwd_grad_in[-1:]], axis=0)
    gate_all = w_gate.reshape(SECTIONS, EXPERTS, D, FF)
    up_all = w_up.reshape(SECTIONS, EXPERTS, D, FF)
    down_all = jnp.transpose(w_down.reshape(SECTIONS, FF, EXPERTS, D), (0, 2, 1, 3))

    def per_section(items):
        inputs, saved, grads, gate_mats, up_mats, down_mats, f_ids, f_gates, b_ids, b_gates = items
        forward_out = forward_section(inputs, f_ids, f_gates, gate_mats, up_mats, down_mats)
        backward_out = backward_section(saved, grads, b_ids, b_gates, gate_mats, up_mats, down_mats)
        return forward_out, backward_out

    fwd_out, bwd_out = lax.map(per_section, (section_x, bwd_in, section_g, gate_all, up_all, down_all, fwd_ids, fwd_gates, bwd_ids, bwd_gates))
    return fwd_out, bwd_out
```

```python
import functools

import jax
import jax.numpy as jnp
from jax import lax
from jax.experimental import pallas as pl
from jax.experimental.pallas import tpu as pltpu
from jax.sharding import PartitionSpec as P

XN = 4
YN = 4
CHUNKS = 4
MESH = pl.DeviceIdType.MESH
NT = (((1,), (1,)), ((), ()))


def kernel(
    sections,
    fwd_slabs,
    bwd_slabs,
    grad_slabs,
    w_gate,
    w_up,
    w_down,
    aux_in,
    fwd_ret,
    bwd_ret,
    gu,
    dn,
    xf,
    xb,
    xg,
    aux,
    xcat,
    gcat,
    s1_out,
    s1_in,
    s2_out,
    s2_in,
    kept,
    s1d_out,
    s1d_in,
    s2d_out,
    s2d_in,
    keptd,
    hid,
    back,
    grads,
    out_acc,
    grad_acc,
    out_send,
    grad_send,
    wdir_send,
    wdir_recv,
    wrel_send,
    wrel_recv,
    wloc,
    disp_send,
    disp_recv,
    s_send,
    s_recv,
    ag_send,
    ag_recv,
    ret_send,
    ret_recv,
):
    section = lax.axis_index("pipe")
    me = lax.axis_index("expert")
    x = me // YN
    y = me % YN
    parity = y % 2
    high = y // 2
    place = parity * 2 + high
    slots = gu.shape[0]
    chunk = dn.shape[3]
    width = dn.shape[2]
    half_rows = width // 2
    full = 2 * width
    last = sections - 1

    def column(k, pipe=None):
        return (section if pipe is None else pipe, x * YN + (y + k) % YN)

    def row(k):
        return (section, (x + k) % XN * YN + y)

    near = (section, x * YN + y + 1 - 2 * parity)
    far = (section, x * YN + (y + 2) % YN)

    barrier = pltpu.get_barrier_semaphore()

    def greet(device):
        pl.semaphore_signal(barrier, inc=1, device_id=device, device_id_type=MESH)

    for k in range(1, YN):
        greet(column(k))
    greet(row(1))
    greet(row(XN - 1))

    @pl.when(section < last)
    def _():
        for k in range(YN):
            greet(column(k, section + 1))

    @pl.when(section > 0)
    def _():
        for k in range(YN):
            greet(column(k, section - 1))

    inner = jnp.where(section < last, YN, 0) + jnp.where(section > 0, YN, 0)
    pl.semaphore_wait(barrier, YN + 1 + inner)

    ending = []

    def send(src, dst, send_sem, recv_sem, device):
        copy = pltpu.make_async_remote_copy(
            src_ref=src,
            dst_ref=dst,
            send_sem=send_sem,
            recv_sem=recv_sem,
            device_id=device,
            device_id_type=MESH,
        )
        copy.start()
        return copy

    def sent(*args):
        ending.append(send(*args))

    def arrive(dst, sem):
        pltpu.make_async_copy(dst, dst, sem).wait()

    items = 2 * slots
    ways = ((1, 0), (XN - 1, 1))

    def parts(i, source):
        f = i % slots
        if i < slots:
            return [gu.at[f, source, :, pl.ds(0, chunk)], gu.at[f, source, :, pl.ds(chunk, chunk)]]
        return [dn.at[f, source]]

    def own_refs(i):
        f = i % slots
        span = pl.ds(f * chunk, chunk)
        if i < slots:
            return [w_gate.at[:, span], w_up.at[:, span]]
        return [w_down.at[:, span]]

    def own_send(i):
        for part, (src, dst) in enumerate(zip(own_refs(i), parts(i, x))):
            for k, way in ways:
                sent(src, dst, wdir_send.at[i, way, part], wdir_recv.at[i, way, part], row(k))

    def direct_wait(i):
        for k, way in ways:
            for part, dst in enumerate(parts(i, (x + XN - k) % XN)):
                arrive(dst, wdir_recv.at[i, way, part])

    def relay_ref(i, source, way):
        f = i % slots
        rows = pl.ds(way * half_rows, half_rows)
        return gu.at[f, source, rows] if i < slots else dn.at[f, source, rows]

    def relay(i):
        for k, way in ways:
            ref = relay_ref(i, (x + XN - k) % XN, way)
            sent(ref, ref, wrel_send.at[i, way], wrel_recv.at[i, way], row(k))

    def relay_wait(i):
        for _, way in ways:
            arrive(relay_ref(i, (x + 2) % XN, way), wrel_recv.at[i, way])

    own_send(0)
    own_send(1)
    locals_ = []
    for i in range(items):
        for part, (src, dst) in enumerate(zip(own_refs(i), parts(i, x))):
            copy = pltpu.make_async_copy(src, dst, wloc.at[i, part])
            copy.start()
            locals_.append((i, copy))

    def spread(number, slabs, buffer, sems_out, sems_in):
        for k in range(1, YN):
            sent(
                slabs.at[(y + k) % YN] if slabs is not aux_in else slabs,
                buffer.at[place],
                sems_out.at[number, k],
                sems_in.at[number, k],
                column(k),
            )
        pltpu.make_async_copy(
            slabs.at[y] if slabs is not aux_in else slabs, buffer.at[place], sems_in.at[number, 0]
        ).start()

    def shifted(number, slabs, buffer, step, edge):
        def copies(target):
            return [
                pltpu.make_async_remote_copy(
                    src_ref=slabs.at[(y + k) % YN],
                    dst_ref=buffer.at[place],
                    send_sem=disp_send.at[number, k],
                    recv_sem=disp_recv.at[number, k],
                    device_id=column(k, target),
                    device_id_type=MESH,
                )
                for k in range(YN)
            ]

        def own():
            return [
                pltpu.make_async_remote_copy(
                    src_ref=slabs.at[(y + k) % YN],
                    dst_ref=buffer.at[place],
                    send_sem=disp_send.at[number, YN + k],
                    recv_sem=disp_recv.at[number, k],
                    device_id=column(k),
                    device_id_type=MESH,
                )
                for k in range(1, YN)
            ]

        stays = last if step > 0 else 0

        @pl.when(section != stays)
        def _():
            for copy in copies(section + step):
                copy.start()

        @pl.when(section == edge)
        def _():
            for copy in own():
                copy.start()
            pltpu.make_async_copy(slabs.at[y], buffer.at[place], disp_recv.at[number, 0]).start()

        def finish():
            @pl.when(section != stays)
            def _():
                for copy in copies(section + step):
                    copy.wait_send()

            @pl.when(section == edge)
            def _():
                for copy in own():
                    copy.wait_send()

        return finish

    def place_of(k):
        other = (y + YN - k) % YN
        return other % 2 * 2 + other // 2

    def spread_wait(number, buffer):
        for k in range(YN):
            arrive(buffer.at[place_of(k)], disp_recv.at[number, k])

    spread(0, aux_in, aux, disp_send, disp_recv)
    fwd_finish = shifted(1, fwd_slabs, xf, 1, 0)
    spread(2, bwd_slabs, xb, disp_send, disp_recv)
    grad_finish = shifted(3, grad_slabs, xg, -1, last)

    direct_wait(0)
    relay(0)
    if items > 2:
        own_send(2)

    spread_wait(0, aux)
    fwd_first = [aux[q, :, 0:1] < 0.5 for q in range(YN)]
    bwd_first = [aux[q, :, 2:3] < 0.5 for q in range(YN)]

    def divide(block, first, target):
        zero = jnp.zeros_like(block)
        target[:, pl.ds(0, full)] = jnp.where(first, block, zero)
        target[:, pl.ds(full, full)] = jnp.where(first, zero, block)

    spread_wait(1, xf)
    for q in range(YN):
        divide(xf[q], fwd_first[q], xcat.at[q // 2, 0, q % 2])
    spread_wait(2, xb)
    for q in range(YN):
        divide(xb[q], bwd_first[q], xcat.at[q // 2, 1, q % 2])

    tokens = xf.shape[1]

    def gather_send(i, ref):
        for k in range(1, YN):
            sent(ref, ref, ag_send.at[i, k - 1], ag_recv.at[i, k - 1], column(k))

    def gather_wait(i, buffer):
        for k in range(1, YN):
            arrive(buffer.at[place_of(k)], ag_recv.at[i, k - 1])

    def first_stage(i):
        f = i % slots
        if i < slots:
            mats = gu[f].reshape(XN * width, 2 * chunk)
            rows = xcat.at[1 - parity][...].reshape(4 * tokens, 2 * full)
            given = jnp.dot(rows, mats, preferred_element_type=jnp.float32)
            s1_out[f] = given.astype(jnp.bfloat16).reshape(s1_out.shape[1:])
            sent(s1_out.at[f], s1_in.at[f], s_send.at[i, 0], s_recv.at[i, 0], near)
            rows = xcat.at[parity][...].reshape(4 * tokens, 2 * full)
            own = jnp.dot(rows, mats, preferred_element_type=jnp.float32)
            kept[f] = own.reshape(kept.shape[1:])
        else:
            mats = dn[f].reshape(XN * width, chunk)
            rows = gcat.at[1 - parity][...].reshape(2 * tokens, 2 * full)
            given = jnp.dot(rows, mats, preferred_element_type=jnp.float32)
            s1d_out[f] = given.astype(jnp.bfloat16).reshape(s1d_out.shape[1:])
            sent(s1d_out.at[f], s1d_in.at[f], s_send.at[i, 0], s_recv.at[i, 0], near)
            rows = gcat.at[parity][...].reshape(2 * tokens, 2 * full)
            own = jnp.dot(rows, mats, preferred_element_type=jnp.float32)
            keptd[f] = own.reshape(keptd.shape[1:])

    def second_stage(i):
        f = i % slots
        if i < slots:
            arrive(s1_in.at[f], s_recv.at[i, 0])
            for b in range(2):
                total = kept[f, b, 1 - high] + s1_in[f, b, 1 - high].astype(jnp.float32)
                s2_out[f, b] = total.astype(jnp.bfloat16)
            sent(s2_out.at[f], s2_in.at[f], s_send.at[i, 1], s_recv.at[i, 1], far)
        else:
            arrive(s1d_in.at[f], s_recv.at[i, 0])
            total = keptd[f, 1 - high] + s1d_in[f, 1 - high].astype(jnp.float32)
            s2d_out[f] = total.astype(jnp.bfloat16)
            sent(s2d_out.at[f], s2d_in.at[f], s_send.at[i, 1], s_recv.at[i, 1], far)

    def third_stage(i):
        f = i % slots
        if i < slots:
            arrive(s2_in.at[f], s_recv.at[i, 1])
            sums = [
                kept[f, b, high]
                + s1_in[f, b, high].astype(jnp.float32)
                + s2_in[f, b].astype(jnp.float32)
                for b in range(2)
            ]
            back[f] = sums[1]
            gate, up = sums[0][:, :chunk], sums[0][:, chunk:]
            hid[f, place] = (gate * jax.nn.sigmoid(gate) * up).astype(jnp.bfloat16)
            gather_send(i, hid.at[f, place])
        else:
            arrive(s2d_in.at[f], s_recv.at[i, 1])
            grad_hidden = (
                keptd[f, high]
                + s1d_in[f, high].astype(jnp.float32)
                + s2d_in[f].astype(jnp.float32)
            )
            gate, up = back[f, :, :chunk], back[f, :, chunk:]
            sig = jax.nn.sigmoid(gate)
            grad_gate = grad_hidden * up * sig * (1.0 + gate * (1.0 - sig))
            grad_up = grad_hidden * (gate * sig)
            grads[f, place, :, pl.ds(0, chunk)] = grad_gate.astype(jnp.bfloat16)
            grads[f, place, :, pl.ds(chunk, chunk)] = grad_up.astype(jnp.bfloat16)
            gather_send(i, grads.at[f, place])

    def accumulate(values, first, mats, acc, start):
        zero = jnp.zeros_like(values[0])
        zeroth = jnp.concatenate([jnp.where(m, v, zero) for m, v in zip(first, values)], axis=0)
        other = jnp.concatenate([jnp.where(m, zero, v) for m, v in zip(first, values)], axis=0)
        total = lax.dot_general(zeroth, mats[:full], NT, preferred_element_type=jnp.float32)
        total += lax.dot_general(other, mats[full:], NT, preferred_element_type=jnp.float32)
        if start:
            acc[...] = total
        else:
            acc[...] += total

    def forward_sum(f):
        gather_wait(f, hid.at[f])
        mats = dn[f].reshape(XN * width, chunk)
        accumulate([hid[f, q] for q in range(YN)], fwd_first, mats, out_acc, f == 0)

    def backward_sum(f):
        gather_wait(slots + f, grads.at[f])
        mats = gu[f].reshape(XN * width, 2 * chunk)
        accumulate([grads[f, q] for q in range(YN)], bwd_first, mats, grad_acc, f == 0)

    def give_back(number, residual, acc, lane, buffer, result):
        for q in range(YN):
            produced = acc[pl.ds(q * tokens, tokens), :].astype(jnp.bfloat16).astype(jnp.float32)
            weight = aux[q, :, lane : lane + 1]
            buffer[q] = (residual[q].astype(jnp.float32) + weight * produced).astype(jnp.bfloat16)
        for k in range(1, YN):
            other = (y + k) % YN
            sent(
                buffer.at[other % 2 * 2 + other // 2],
                result.at[y],
                ret_send.at[number, k],
                ret_recv.at[number, k],
                column(k),
            )
        pltpu.make_async_copy(buffer.at[place], result.at[y], ret_recv.at[number, 0]).start()

    def give_wait(number, result):
        for k in range(YN):
            arrive(result.at[(y + YN - k) % YN], ret_recv.at[number, k])

    for i in range(items):
        f = i % slots
        if i + 1 < items:
            direct_wait(i + 1)
            relay(i + 1)
            if i + 3 < items:
                own_send(i + 3)
        relay_wait(i)
        for number, copy in locals_:
            if number == i:
                copy.wait()
        if i == slots:
            spread_wait(3, xg)
            for q in range(YN):
                divide(xg[q], bwd_first[q], gcat.at[q // 2, q % 2])
        first_stage(i)
        if i > 0:
            third_stage(i - 1)
        if i >= slots and f >= 1:
            forward_sum(f - 1)
        second_stage(i)
        if i >= slots and f >= 2:
            backward_sum(f - 2)

    forward_sum(slots - 1)
    third_stage(items - 1)
    give_back(0, xf, out_acc, 1, out_send, fwd_ret)
    if slots >= 2:
        backward_sum(slots - 2)
    backward_sum(slots - 1)
    give_back(1, xg, grad_acc, 3, grad_send, bwd_ret)
    give_wait(0, fwd_ret)
    give_wait(1, bwd_ret)
    for copy in ending:
        copy.wait_send()
    fwd_finish()
    grad_finish()


def fused(fwd_slabs, bwd_slabs, grad_slabs, w_gate, w_up, w_down, aux, sections):
    _, tokens, full = fwd_slabs.shape
    width, units = w_gate.shape
    slots = CHUNKS
    chunk = units // slots
    rows = YN * tokens
    bf16, f32 = jnp.bfloat16, jnp.float32
    dma = pltpu.SemaphoreType.DMA
    items = 2 * slots
    slab = jax.ShapeDtypeStruct((YN, tokens, full), bf16)
    return pl.pallas_call(
        functools.partial(kernel, sections),
        out_shape=(slab, slab),
        in_specs=[pl.BlockSpec(memory_space=pl.ANY)] * 7,
        out_specs=(pl.BlockSpec(memory_space=pl.ANY),) * 2,
        scratch_shapes=[
            pltpu.VMEM((slots, XN, width, 2 * chunk), bf16),
            pltpu.VMEM((slots, XN, width, chunk), bf16),
            pltpu.VMEM((YN, tokens, full), bf16),
            pltpu.VMEM((YN, tokens, full), bf16),
            pltpu.VMEM((YN, tokens, full), bf16),
            pltpu.VMEM((YN, tokens, 128), f32),
            pltpu.VMEM((2, 2, 2, tokens, 2 * full), bf16),
            pltpu.VMEM((2, 2, tokens, 2 * full), bf16),
            pltpu.VMEM((slots, 2, 2, tokens, 2 * chunk), bf16),
            pltpu.VMEM((slots, 2, 2, tokens, 2 * chunk), bf16),
            pltpu.VMEM((slots, 2, tokens, 2 * chunk), bf16),
            pltpu.VMEM((slots, 2, tokens, 2 * chunk), bf16),
            pltpu.VMEM((slots, 2, 2, tokens, 2 * chunk), f32),
            pltpu.VMEM((slots, 2, tokens, chunk), bf16),
            pltpu.VMEM((slots, 2, tokens, chunk), bf16),
            pltpu.VMEM((slots, tokens, chunk), bf16),
            pltpu.VMEM((slots, tokens, chunk), bf16),
            pltpu.VMEM((slots, 2, tokens, chunk), f32),
            pltpu.VMEM((slots, YN, tokens, chunk), bf16),
            pltpu.VMEM((slots, tokens, 2 * chunk), f32),
            pltpu.VMEM((slots, YN, tokens, 2 * chunk), bf16),
            pltpu.VMEM((rows, full), f32),
            pltpu.VMEM((rows, full), f32),
            pltpu.VMEM((YN, tokens, full), bf16),
            pltpu.VMEM((YN, tokens, full), bf16),
            dma((items, 2, 2)),
            dma((items, 2, 2)),
            dma((items, 2)),
            dma((items, 2)),
            dma((items, 2)),
            dma((4, 2 * YN)),
            dma((4, YN)),
            dma((items, 2)),
            dma((items, 2)),
            dma((items, YN - 1)),
            dma((items, YN - 1)),
            dma((2, YN)),
            dma((2, YN)),
        ],
        compiler_params=pltpu.CompilerParams(
            collective_id=0, has_side_effects=True, vmem_limit_bytes=62 * 1024 * 1024
        ),
    )(fwd_slabs, bwd_slabs, grad_slabs, w_gate, w_up, w_down, aux)


def slabs_of(values):
    tokens, model = values.shape
    cut = values.reshape(tokens, 2, YN, model // (2 * YN))
    return cut.transpose(2, 0, 1, 3).reshape(YN, tokens, model // YN)


def whole_of(slabs):
    _, tokens, full = slabs.shape
    cut = slabs.reshape(YN, tokens, 2, full // 2)
    return cut.transpose(1, 2, 0, 3).reshape(tokens, YN * full)


def body(sections, fwd_in, bwd_in, bwd_grad_in, w_gate, w_up, w_down, fwd_ids, fwd_gates, bwd_ids, bwd_gates):
    f32 = jnp.float32
    aux = jnp.concatenate(
        [fwd_ids[0].astype(f32), fwd_gates[0], bwd_ids[0].astype(f32), bwd_gates[0]], axis=1
    )
    aux = jnp.pad(aux, ((0, 0), (0, 124)))
    fwd, bwd = fused(
        slabs_of(fwd_in[0]),
        slabs_of(bwd_in[0]),
        slabs_of(bwd_grad_in[0]),
        w_gate[0],
        w_up[0],
        w_down[0].T,
        aux,
        sections,
    )
    return whole_of(fwd)[None], whole_of(bwd)[None]


def solution(mesh):
    rows = P("pipe", "expert", None)
    return jax.shard_map(
        functools.partial(body, mesh.shape["pipe"]),
        mesh=mesh,
        in_specs=(rows, rows, rows, rows, rows, P("pipe", None, "expert"), rows, rows, rows, rows),
        out_specs=(rows, rows),
        check_vma=False,
    )
```

```python
import functools

import jax
import jax.numpy as jnp
from jax import lax
from jax.experimental import pallas as pl
from jax.experimental.pallas import tpu as pltpu
from jax.sharding import PartitionSpec as P

XN = 4
YN = 4
GATE_PARTS = (2, 2, 2, 2)
DOWN_PARTS = (2, 2, 2, 1, 1)
MESH = pl.DeviceIdType.MESH
NT = (((1,), (1,)), ((), ()))


class Chunk:
    def __init__(self, start, size, parent=None):
        self.start, self.size, self.parent = start, size, parent


def chunks_of(units):
    step = units // sum(GATE_PARTS)
    gates, start = [], 0
    for size in GATE_PARTS:
        gates.append(Chunk(start * step, size * step))
        start += size
    downs, start = [], 0
    for size in DOWN_PARTS:
        first = start * step
        parent = [n for n, g in enumerate(gates) if g.start <= first < g.start + g.size][0]
        downs.append(Chunk(first, size * step, parent))
        start += size
    return gates, downs


def kernel(sections, gates, downs, *refs):
    (fwd_in, bwd_in, grad_in, w_gate, w_up, w_down, fwd_ids, fwd_gates, bwd_ids, bwd_gates) = refs[:10]
    fwd_out, bwd_out = refs[10:12]
    refs = refs[12:]

    def take(count):
        nonlocal refs
        taken, refs = refs[:count], refs[count:]
        return taken

    ng, nd = len(gates), len(downs)
    gu, s1_out, s1_in, s2_out, s2_in, kept, hid, back = [take(ng) for _ in range(8)]
    dn, s1d_out, s1d_in, s2d_out, s2d_in, keptd, grads = [take(nd) for _ in range(7)]
    (whole, small, slab, aux_in, aux, land, xcat, gcat) = take(8)
    (out_acc, grad_acc, ret_out, ret_in) = take(4)
    (load, wdir_send, wdir_recv, wrel_send, wrel_recv, wloc) = take(6)
    (disp_send, disp_recv, s_send, s_recv, ag_send, ag_recv, ret_send, ret_recv, store) = take(9)
    xf, xb, xg = land.at[0], land.at[1], land.at[2]

    section = lax.axis_index("pipe")
    me = lax.axis_index("expert")
    x = me // YN
    y = me % YN
    parity = y % 2
    high = y // 2
    place = parity * 2 + high
    tokens = fwd_in.shape[0]
    width = w_gate.shape[0]
    half_rows = width // 2
    full = 2 * width
    last = sections - 1

    loads = []
    for n, (src, dst) in enumerate(
        [(fwd_in, whole.at[0]), (bwd_in, whole.at[1]), (grad_in, whole.at[2])]
        + [(ref, small.at[j]) for j, ref in enumerate((fwd_ids, fwd_gates, bwd_ids, bwd_gates))]
    ):
        loads.append(pltpu.make_async_copy(src, dst, load.at[n]))
        loads[-1].start()

    def column(k, pipe=None):
        return (section if pipe is None else pipe, x * YN + (y + k) % YN)

    def row(k):
        return (section, (x + k) % XN * YN + y)

    near = (section, x * YN + y + 1 - 2 * parity)
    far = (section, x * YN + (y + 2) % YN)

    barrier = pltpu.get_barrier_semaphore()

    def greet(device):
        pl.semaphore_signal(barrier, inc=1, device_id=device, device_id_type=MESH)

    @pl.when(section < last)
    def _():
        for k in range(YN):
            greet(column(k, section + 1))

    @pl.when(section > 0)
    def _():
        for k in range(YN):
            greet(column(k, section - 1))

    for k in range(1, YN):
        greet(column(k))
    greet(row(1))
    greet(row(XN - 1))

    def cut(n):
        loads[n].wait()
        for t in range(YN):
            slab[n, t] = jnp.concatenate(
                [
                    whole[n, :, t * width : (t + 1) * width],
                    whole[n, :, (YN + t) * width : (YN + t + 1) * width],
                ],
                axis=1,
            )

    for n in range(3, 7):
        loads[n].wait()
    eye = lax.broadcasted_iota(jnp.int32, (tokens, tokens), 0) == lax.broadcasted_iota(
        jnp.int32, (tokens, tokens), 1
    )
    lane = lax.broadcasted_iota(jnp.int32, (tokens, 128), 1)
    table = jnp.zeros((tokens, 128), jnp.float32)
    for j in range(4):
        line = jnp.broadcast_to(small[j], (tokens, tokens))
        stood = jnp.sum(jnp.where(eye, line, 0.0), axis=1, keepdims=True)
        table = jnp.where(lane == j, stood, table)
    aux_in[...] = table
    cut(0)
    cut(1)

    inner = jnp.where(section < last, YN, 0) + jnp.where(section > 0, YN, 0)
    pl.semaphore_wait(barrier, YN + 1 + inner)

    ending = []

    def send(src, dst, send_sem, recv_sem, device):
        copy = pltpu.make_async_remote_copy(
            src_ref=src,
            dst_ref=dst,
            send_sem=send_sem,
            recv_sem=recv_sem,
            device_id=device,
            device_id_type=MESH,
        )
        copy.start()
        return copy

    def sent(*args):
        ending.append(send(*args))

    def arrive(dst, sem):
        pltpu.make_async_copy(dst, dst, sem).wait()

    items = ng + nd
    ways = ((1, 0), (XN - 1, 1))

    def parts(i, source):
        if i < ng:
            c = gates[i].size
            return [gu[i].at[source, :, pl.ds(0, c)], gu[i].at[source, :, pl.ds(c, c)]]
        return [dn[i - ng].at[source]]

    def own_refs(i):
        c = gates[i] if i < ng else downs[i - ng]
        span = pl.ds(c.start, c.size)
        return [w_gate.at[:, span], w_up.at[:, span]] if i < ng else [w_down.at[:, span]]

    def own_send(i):
        if i >= items:
            return
        for part, (src, dst) in enumerate(zip(own_refs(i), parts(i, x))):
            for k, way in ways:
                sent(src, dst, wdir_send.at[i, way, part], wdir_recv.at[i, way, part], row(k))

    def direct_wait(i):
        for k, way in ways:
            for part, dst in enumerate(parts(i, (x + XN - k) % XN)):
                arrive(dst, wdir_recv.at[i, way, part])

    def relay_ref(i, source, way):
        rows = pl.ds(way * half_rows, half_rows)
        return gu[i].at[source, rows] if i < ng else dn[i - ng].at[source, rows]

    def relay(i):
        for k, way in ways:
            ref = relay_ref(i, (x + XN - k) % XN, way)
            sent(ref, ref, wrel_send.at[i, way], wrel_recv.at[i, way], row(k))

    def relay_wait(i):
        for _, way in ways:
            arrive(relay_ref(i, (x + 2) % XN, way), wrel_recv.at[i, way])

    own_send(0)
    own_send(1)

    def spread(number, source, buffer):
        for k in range(1, YN):
            sent(
                source(k),
                buffer.at[place],
                disp_send.at[number, k],
                disp_recv.at[number, k],
                column(k),
            )
        pltpu.make_async_copy(source(0), buffer.at[place], disp_recv.at[number, 0]).start()

    def shifted(number, n, buffer, step, edge):
        def copies(target):
            return [
                pltpu.make_async_remote_copy(
                    src_ref=slab.at[n, (y + k) % YN],
                    dst_ref=buffer.at[place],
                    send_sem=disp_send.at[number, k],
                    recv_sem=disp_recv.at[number, k],
                    device_id=column(k, target),
                    device_id_type=MESH,
                )
                for k in range(YN)
            ]

        def own():
            return [
                pltpu.make_async_remote_copy(
                    src_ref=slab.at[n, (y + k) % YN],
                    dst_ref=buffer.at[place],
                    send_sem=disp_send.at[number, YN + k],
                    recv_sem=disp_recv.at[number, k],
                    device_id=column(k),
                    device_id_type=MESH,
                )
                for k in range(1, YN)
            ]

        stays = last if step > 0 else 0

        @pl.when(section != stays)
        def _():
            for copy in copies(section + step):
                copy.start()

        @pl.when(section == edge)
        def _():
            for copy in own():
                copy.start()
            pltpu.make_async_copy(slab.at[n, y], buffer.at[place], disp_recv.at[number, 0]).start()

        def finish():
            @pl.when(section != stays)
            def _():
                for copy in copies(section + step):
                    copy.wait_send()

            @pl.when(section == edge)
            def _():
                for copy in own():
                    copy.wait_send()

        return finish

    def place_of(k):
        other = (y + YN - k) % YN
        return other % 2 * 2 + other // 2

    def spread_wait(number, buffer):
        for k in range(YN):
            arrive(buffer.at[place_of(k)], disp_recv.at[number, k])

    spread(0, lambda k: aux_in, aux)
    fwd_finish = shifted(1, 0, xf, 1, 0)
    spread(2, lambda k: slab.at[1, (y + k) % YN], xb)

    locals_ = []
    for i in range(items):
        for part, (src, dst) in enumerate(zip(own_refs(i), parts(i, x))):
            copy = pltpu.make_async_copy(src, dst, wloc.at[i, part])
            copy.start()
            locals_.append((i, copy))

    cut(2)
    grad_finish = shifted(3, 2, xg, -1, last)

    direct_wait(0)
    relay(0)
    own_send(2)

    spread_wait(0, aux)
    fwd_first = [aux[q, :, 0:1] < 0.5 for q in range(YN)]
    bwd_first = [aux[q, :, 2:3] < 0.5 for q in range(YN)]

    def divide(block, first, target):
        zero = jnp.zeros_like(block)
        target[:, pl.ds(0, full)] = jnp.where(first, block, zero)
        target[:, pl.ds(full, full)] = jnp.where(first, zero, block)

    spread_wait(1, xf)
    for q in range(YN):
        divide(xf[q], fwd_first[q], xcat.at[q // 2, 0, q % 2])
    spread_wait(2, xb)
    for q in range(YN):
        divide(xb[q], bwd_first[q], xcat.at[q // 2, 1, q % 2])

    def gather_send(i, ref):
        for k in (2, 1, 3):
            sent(ref, ref, ag_send.at[i, k - 1], ag_recv.at[i, k - 1], column(k))

    def gather_wait(i, buffer):
        for k in range(1, YN):
            arrive(buffer.at[place_of(k)], ag_recv.at[i, k - 1])

    def first_stage(i):
        if i < ng:
            mats = gu[i][...].reshape(XN * width, 2 * gates[i].size)
            source, out, into, keep, count = xcat, s1_out[i], s1_in[i], kept[i], 4
        else:
            d = i - ng
            mats = dn[d][...].reshape(XN * width, downs[d].size)
            source, out, into, keep, count = gcat, s1d_out[d], s1d_in[d], keptd[d], 2
        rows = source.at[1 - parity][...].reshape(count * tokens, 2 * full)
        given = jnp.dot(rows, mats, preferred_element_type=jnp.float32)
        out[...] = given.astype(jnp.bfloat16).reshape(out.shape)
        sent(out, into, s_send.at[i, 0], s_recv.at[i, 0], near)
        rows = source.at[parity][...].reshape(count * tokens, 2 * full)
        own = jnp.dot(rows, mats, preferred_element_type=jnp.float32)
        keep[...] = own.reshape(keep.shape)

    def second_stage(i):
        if i < ng:
            arrive(s1_in[i], s_recv.at[i, 0])
            for b in range(2):
                total = kept[i][b, 1 - high] + s1_in[i][b, 1 - high].astype(jnp.float32)
                s2_out[i][b] = total.astype(jnp.bfloat16)
            sent(s2_out[i], s2_in[i], s_send.at[i, 1], s_recv.at[i, 1], far)
        else:
            d = i - ng
            arrive(s1d_in[d], s_recv.at[i, 0])
            total = keptd[d][1 - high] + s1d_in[d][1 - high].astype(jnp.float32)
            s2d_out[d][...] = total.astype(jnp.bfloat16)
            sent(s2d_out[d], s2d_in[d], s_send.at[i, 1], s_recv.at[i, 1], far)

    def third_stage(i):
        if i < ng:
            c = gates[i].size
            arrive(s2_in[i], s_recv.at[i, 1])
            sums = [
                kept[i][b, high]
                + s1_in[i][b, high].astype(jnp.float32)
                + s2_in[i][b].astype(jnp.float32)
                for b in range(2)
            ]
            back[i][...] = sums[1]
            gate, up = sums[0][:, :c], sums[0][:, c:]
            hid[i][place] = (gate * jax.nn.sigmoid(gate) * up).astype(jnp.bfloat16)
            gather_send(i, hid[i].at[place])
        else:
            d = i - ng
            c, home = downs[d].size, downs[d].parent
            at = downs[d].start - gates[home].start
            arrive(s2d_in[d], s_recv.at[i, 1])
            grad_hidden = (
                keptd[d][high]
                + s1d_in[d][high].astype(jnp.float32)
                + s2d_in[d][...].astype(jnp.float32)
            )
            gate = back[home][:, at : at + c]
            up = back[home][:, gates[home].size + at : gates[home].size + at + c]
            sig = jax.nn.sigmoid(gate)
            grad_gate = grad_hidden * up * sig * (1.0 + gate * (1.0 - sig))
            grad_up = grad_hidden * (gate * sig)
            grads[d][place, :, pl.ds(0, c)] = grad_gate.astype(jnp.bfloat16)
            grads[d][place, :, pl.ds(c, c)] = grad_up.astype(jnp.bfloat16)
            gather_send(i, grads[d].at[place])

    def accumulate(values, first, mats, acc, start):
        zero = jnp.zeros_like(values[0])
        zeroth = jnp.concatenate([jnp.where(m, v, zero) for m, v in zip(first, values)], axis=0)
        other = jnp.concatenate([jnp.where(m, zero, v) for m, v in zip(first, values)], axis=0)
        total = lax.dot_general(zeroth, mats[:full], NT, preferred_element_type=jnp.float32)
        total += lax.dot_general(other, mats[full:], NT, preferred_element_type=jnp.float32)
        if start:
            acc[...] = total
        else:
            acc[...] += total

    def forward_sum(d):
        c, home = downs[d].size, downs[d].parent
        at = downs[d].start - gates[home].start
        if at == 0:
            gather_wait(home, hid[home])
        mats = dn[d][...].reshape(XN * width, c)
        values = [hid[home][q, :, at : at + c] for q in range(YN)]
        accumulate(values, fwd_first, mats, out_acc, d == 0)

    def backward_sum(d):
        c, home = downs[d].size, downs[d].parent
        at, size = downs[d].start - gates[home].start, gates[home].size
        gather_wait(ng + d, grads[d])
        mats = gu[home][...].reshape(XN * width, 2 * size)
        if c != size:
            mats = jnp.concatenate([mats[:, at : at + c], mats[:, size + at : size + at + c]], axis=1)
        accumulate([grads[d][q] for q in range(YN)], bwd_first, mats, grad_acc, d == 0)

    pieces = 2
    span = tokens // pieces

    def finished(number, q, residual, acc, where_lane):
        produced = acc[pl.ds(q * tokens, tokens), :].astype(jnp.bfloat16).astype(jnp.float32)
        weight = aux[q, :, where_lane : where_lane + 1]
        return (residual[q].astype(jnp.float32) + weight * produced).astype(jnp.bfloat16)

    def give(number, residual, acc, where_lane):
        for q in range(YN):
            ret_out[number, q] = finished(number, q, residual, acc, where_lane)

    def give_send(number, piece):
        rows = pl.ds(piece * span, span)
        for k in (2, 1, 3):
            other = (y + k) % YN
            sent(
                ret_out.at[number, other % 2 * 2 + other // 2, rows],
                ret_in.at[number, y, rows],
                ret_send.at[number, piece, k],
                ret_recv.at[number, piece, k],
                column(k),
            )

    def give_own(number):
        ret_in[number, y] = ret_out[number, place]

    stores = []

    def collect(number, result):
        for piece in range(pieces):
            rows = pl.ds(piece * span, span)
            for k in range(1, YN):
                other = (y + YN - k) % YN
                arrive(ret_in.at[number, other, rows], ret_recv.at[number, piece, k])
        whole[number] = jnp.concatenate(
            [ret_in[number, t, :, h * width : (h + 1) * width] for h in range(2) for t in range(YN)],
            axis=1,
        )
        stores.append(pltpu.make_async_copy(whole.at[number], result, store.at[number]))
        stores[-1].start()

    for i in range(items):
        d = i - ng
        if i + 1 < items:
            direct_wait(i + 1)
            relay(i + 1)
            own_send(i + 3)
        relay_wait(i)
        for number, copy in locals_:
            if number == i:
                copy.wait()
        if i == ng:
            spread_wait(3, xg)
            for q in range(YN):
                divide(xg[q], bwd_first[q], gcat.at[q // 2, q % 2])
        first_stage(i)
        if i > 0:
            third_stage(i - 1)
        if d >= 1:
            forward_sum(d - 1)
        if d == nd - 1:
            forward_sum(d)
            give(0, xf, out_acc, 1)
        second_stage(i)
        if d >= 2:
            backward_sum(d - 2)

    give_send(0, 0)
    give_own(0)
    if nd >= 2:
        backward_sum(nd - 2)
    third_stage(items - 1)
    give_send(0, 1)
    backward_sum(nd - 1)
    give(1, xg, grad_acc, 3)
    give_send(1, 0)
    give_send(1, 1)
    give_own(1)
    collect(0, fwd_out)
    fwd_finish()
    grad_finish()
    for copy in ending:
        copy.wait_send()
    collect(1, bwd_out)
    for copy in stores:
        copy.wait()


def fused(arrays, sections):
    tokens, model = arrays[0].shape
    width, units = arrays[3].shape
    gates, downs = chunks_of(units)
    full = model // YN
    bf16, f32 = jnp.bfloat16, jnp.float32
    dma = pltpu.SemaphoreType.DMA
    items = len(gates) + len(downs)
    whole = jax.ShapeDtypeStruct((tokens, model), bf16)
    ups = [2 * c.size for c in gates]
    sizes = [c.size for c in downs]

    def each(lead, tail, counts, kind):
        return [pltpu.VMEM(lead + (n,) + tail, kind) for n in counts]

    scratch = []
    scratch += each((XN, width), (), ups, bf16)
    scratch += each((2, 2, tokens), (), ups, bf16)
    scratch += each((2, 2, tokens), (), ups, bf16)
    scratch += each((2, tokens), (), ups, bf16)
    scratch += each((2, tokens), (), ups, bf16)
    scratch += each((2, 2, tokens), (), ups, f32)
    scratch += each((YN, tokens), (), [n // 2 for n in ups], bf16)
    scratch += each((tokens,), (), ups, f32)
    scratch += each((XN, width), (), sizes, bf16)
    scratch += each((2, tokens), (), sizes, bf16)
    scratch += each((2, tokens), (), sizes, bf16)
    scratch += each((tokens,), (), sizes, bf16)
    scratch += each((tokens,), (), sizes, bf16)
    scratch += each((2, tokens), (), sizes, f32)
    scratch += each((YN, tokens), (), [2 * n for n in sizes], bf16)
    scratch += [
        pltpu.VMEM((3, tokens, model), bf16),
        pltpu.VMEM((4, 1, tokens), f32),
        pltpu.VMEM((3, YN, tokens, full), bf16),
        pltpu.VMEM((tokens, 128), f32),
        pltpu.VMEM((YN, tokens, 128), f32),
        pltpu.VMEM((3, YN, tokens, full), bf16),
        pltpu.VMEM((2, 2, 2, tokens, 2 * full), bf16),
        pltpu.VMEM((2, 2, tokens, 2 * full), bf16),
        pltpu.VMEM((YN * tokens, full), f32),
        pltpu.VMEM((YN * tokens, full), f32),
        pltpu.VMEM((2, YN, tokens, full), bf16),
        pltpu.VMEM((2, YN, tokens, full), bf16),
        dma((7,)),
        dma((items, 2, 2)),
        dma((items, 2, 2)),
        dma((items, 2)),
        dma((items, 2)),
        dma((items, 2)),
        dma((4, 2 * YN)),
        dma((4, YN)),
        dma((items, 2)),
        dma((items, 2)),
        dma((items, YN - 1)),
        dma((items, YN - 1)),
        dma((2, 2, YN)),
        dma((2, 2, YN)),
        dma((2,)),
    ]
    return pl.pallas_call(
        functools.partial(kernel, sections, gates, downs),
        out_shape=(whole, whole),
        in_specs=[pl.BlockSpec(memory_space=pl.ANY)] * 10,
        out_specs=(pl.BlockSpec(memory_space=pl.ANY),) * 2,
        scratch_shapes=scratch,
        compiler_params=pltpu.CompilerParams(
            collective_id=0, has_side_effects=True, vmem_limit_bytes=62 * 1024 * 1024
        ),
    )(*arrays)


def body(sections, fwd_in, bwd_in, bwd_grad_in, w_gate, w_up, w_down, fwd_ids, fwd_gates, bwd_ids, bwd_gates):
    def line(values):
        return values.astype(jnp.float32).reshape(1, -1)

    arrays = [fwd_in[0], bwd_in[0], bwd_grad_in[0], w_gate[0], w_up[0], w_down[0].T]
    arrays += [line(fwd_ids), line(fwd_gates), line(bwd_ids), line(bwd_gates)]
    fwd, bwd = fused(arrays, sections)
    return fwd[None], bwd[None]


def solution(mesh):
    rows = P("pipe", "expert", None)
    return jax.shard_map(
        functools.partial(body, mesh.shape["pipe"]),
        mesh=mesh,
        in_specs=(rows, rows, rows, rows, rows, P("pipe", None, "expert"), rows, rows, rows, rows),
        out_specs=(rows, rows),
        check_vma=False,
    )
```

```python
import functools

import jax
import jax.numpy as jnp
from jax import lax
from jax.experimental import pallas as pl
from jax.experimental.pallas import tpu as pltpu
from jax.sharding import PartitionSpec as P

XN = 4
YN = 4
GATE_PARTS = (2, 2, 2, 2)
DOWN_PARTS = (2, 2, 2, 1, 1)
MESH = pl.DeviceIdType.MESH
NT = (((1,), (1,)), ((), ()))


class Chunk:
    def __init__(self, start, size, parent=None):
        self.start, self.size, self.parent = start, size, parent


def chunks_of(units):
    step = units // sum(GATE_PARTS)
    gates, start = [], 0
    for size in GATE_PARTS:
        gates.append(Chunk(start * step, size * step))
        start += size
    downs, start = [], 0
    for size in DOWN_PARTS:
        first = start * step
        parent = [n for n, g in enumerate(gates) if g.start <= first < g.start + g.size][0]
        downs.append(Chunk(first, size * step, parent))
        start += size
    return gates, downs


def kernel(sections, gates, downs, *refs):
    (fwd_in, bwd_in, grad_in, w_gate, w_up, w_down, fwd_ids, fwd_gates, bwd_ids, bwd_gates) = refs[:10]
    fwd_out, bwd_out = refs[10:12]
    refs = refs[12:]

    def take(count):
        nonlocal refs
        taken, refs = refs[:count], refs[count:]
        return taken

    ng, nd = len(gates), len(downs)
    gu, s1_out, s1_in, s2_out, s2_in, kept, hid, back = [take(ng) for _ in range(8)]
    dn, s1d_out, s1d_in, s2d_out, s2d_in, keptd, grads = [take(nd) for _ in range(7)]
    (whole, ids, weights, slab, aux_in, aux, land, xcat, gcat) = take(9)
    (out_acc, grad_acc, ret_out, ret_in) = take(4)
    (load, wdir_send, wdir_recv, wrel_send, wrel_recv, wloc) = take(6)
    (disp_send, disp_recv, s_send, s_recv, ag_send, ag_recv, ret_send, ret_recv, store) = take(9)
    xf, xb, xg = land.at[0], land.at[1], land.at[2]

    section = lax.axis_index("pipe")
    me = lax.axis_index("expert")
    x = me // YN
    y = me % YN
    place = y
    half = y // 2
    rest = 1 - half
    inner = (y == 1) | (y == 2)
    outer = (y == 0) | (y == 3)
    tokens = fwd_in.shape[0]
    width = w_gate.shape[0]
    half_rows = width // 2
    full = 2 * width
    last = sections - 1

    loads = []
    for n, (src, dst) in enumerate(
        [(fwd_in, whole.at[0]), (bwd_in, whole.at[1]), (grad_in, whole.at[2])]
        + [(fwd_ids, ids.at[0]), (fwd_gates, weights.at[0])]
        + [(bwd_ids, ids.at[1]), (bwd_gates, weights.at[1])]
    ):
        loads.append(pltpu.make_async_copy(src, dst, load.at[n]))
        loads[-1].start()

    def column(k, pipe=None):
        return (section if pipe is None else pipe, x * YN + (y + k) % YN)

    def row(k):
        return (section, (x + k) % XN * YN + y)

    my_inner = (section, x * YN + 1 + half)
    my_outer = (section, x * YN + 3 * half)
    far_outer = (section, x * YN + 3 - 3 * half)
    across = (section, x * YN + 2 - half)

    barrier = pltpu.get_barrier_semaphore()

    def greet(device):
        pl.semaphore_signal(barrier, inc=1, device_id=device, device_id_type=MESH)

    @pl.when(section < last)
    def _():
        for k in range(YN):
            greet(column(k, section + 1))

    @pl.when(section > 0)
    def _():
        for k in range(YN):
            greet(column(k, section - 1))

    for k in range(1, YN):
        greet(column(k))
    greet(row(1))
    greet(row(XN - 1))

    def cut(n):
        loads[n].wait()
        for t in range(YN):
            slab[n, t] = jnp.concatenate(
                [
                    whole[n, :, t * width : (t + 1) * width],
                    whole[n, :, (YN + t) * width : (YN + t + 1) * width],
                ],
                axis=1,
            )

    for n in range(3, 7):
        loads[n].wait()
    eye = lax.broadcasted_iota(jnp.int32, (tokens, tokens), 0) == lax.broadcasted_iota(
        jnp.int32, (tokens, tokens), 1
    )
    lane = lax.broadcasted_iota(jnp.int32, (tokens, 128), 1)
    table = jnp.zeros((tokens, 128), jnp.float32)
    for j in range(4):
        line = (weights if j % 2 else ids)[j // 2].astype(jnp.float32)
        line = jnp.broadcast_to(line, (tokens, tokens))
        stood = jnp.sum(jnp.where(eye, line, 0.0), axis=1, keepdims=True)
        table = jnp.where(lane == j, stood, table)
    aux_in[...] = table
    cut(0)
    cut(1)

    others = jnp.where(section < last, YN, 0) + jnp.where(section > 0, YN, 0)
    pl.semaphore_wait(barrier, YN + 1 + others)

    ending, inner_ending, outer_ending = [], [], []

    def remote(src, dst, send_sem, recv_sem, device):
        return pltpu.make_async_remote_copy(
            src_ref=src,
            dst_ref=dst,
            send_sem=send_sem,
            recv_sem=recv_sem,
            device_id=device,
            device_id_type=MESH,
        )

    def sent(*args):
        copy = remote(*args)
        copy.start()
        ending.append(copy)

    def sent_by(end, args):
        remote(*args()).start()
        end.append(args)

    def arrive(dst, sem):
        pltpu.make_async_copy(dst, dst, sem).wait()

    items = ng + nd
    ways = ((1, 0), (XN - 1, 1))

    def parts(i, source):
        if i < ng:
            c = gates[i].size
            return [gu[i].at[source, :, pl.ds(0, c)], gu[i].at[source, :, pl.ds(c, c)]]
        return [dn[i - ng].at[source]]

    def own_refs(i):
        c = gates[i] if i < ng else downs[i - ng]
        span = pl.ds(c.start, c.size)
        return [w_gate.at[:, span], w_up.at[:, span]] if i < ng else [w_down.at[:, span]]

    def own_send(i):
        if i >= items:
            return
        for part, (src, dst) in enumerate(zip(own_refs(i), parts(i, x))):
            for k, way in ways:
                sent(src, dst, wdir_send.at[i, way, part], wdir_recv.at[i, way, part], row(k))

    def direct_wait(i):
        for k, way in ways:
            for part, dst in enumerate(parts(i, (x + XN - k) % XN)):
                arrive(dst, wdir_recv.at[i, way, part])

    def relay_ref(i, source, way):
        rows = pl.ds(way * half_rows, half_rows)
        return gu[i].at[source, rows] if i < ng else dn[i - ng].at[source, rows]

    def relay(i):
        for k, way in ways:
            ref = relay_ref(i, (x + XN - k) % XN, way)
            sent(ref, ref, wrel_send.at[i, way], wrel_recv.at[i, way], row(k))

    def relay_wait(i):
        for _, way in ways:
            arrive(relay_ref(i, (x + 2) % XN, way), wrel_recv.at[i, way])

    own_send(0)
    own_send(1)

    def spread(number, source, buffer):
        for k in range(1, YN):
            sent(
                source(k),
                buffer.at[place],
                disp_send.at[number, k],
                disp_recv.at[number, k],
                column(k),
            )
        pltpu.make_async_copy(source(0), buffer.at[place], disp_recv.at[number, 0]).start()

    def shifted(number, n, buffer, step, edge):
        def copies(target):
            return [
                pltpu.make_async_remote_copy(
                    src_ref=slab.at[n, (y + k) % YN],
                    dst_ref=buffer.at[place],
                    send_sem=disp_send.at[number, k],
                    recv_sem=disp_recv.at[number, k],
                    device_id=column(k, target),
                    device_id_type=MESH,
                )
                for k in range(YN)
            ]

        def own():
            return [
                pltpu.make_async_remote_copy(
                    src_ref=slab.at[n, (y + k) % YN],
                    dst_ref=buffer.at[place],
                    send_sem=disp_send.at[number, YN + k],
                    recv_sem=disp_recv.at[number, k],
                    device_id=column(k),
                    device_id_type=MESH,
                )
                for k in range(1, YN)
            ]

        stays = last if step > 0 else 0

        @pl.when(section != stays)
        def _():
            for copy in copies(section + step):
                copy.start()

        @pl.when(section == edge)
        def _():
            for copy in own():
                copy.start()
            pltpu.make_async_copy(slab.at[n, y], buffer.at[place], disp_recv.at[number, 0]).start()

        def finish():
            @pl.when(section != stays)
            def _():
                for copy in copies(section + step):
                    copy.wait_send()

            @pl.when(section == edge)
            def _():
                for copy in own():
                    copy.wait_send()

        return finish

    def place_of(k):
        return (y + YN - k) % YN

    def spread_wait(number, buffer):
        for k in range(YN):
            arrive(buffer.at[place_of(k)], disp_recv.at[number, k])

    spread(0, lambda k: aux_in, aux)
    fwd_finish = shifted(1, 0, xf, 1, 0)
    spread(2, lambda k: slab.at[1, (y + k) % YN], xb)

    locals_ = []
    for i in range(items):
        for part, (src, dst) in enumerate(zip(own_refs(i), parts(i, x))):
            copy = pltpu.make_async_copy(src, dst, wloc.at[i, part])
            copy.start()
            locals_.append((i, copy))

    cut(2)
    grad_finish = shifted(3, 2, xg, -1, last)

    direct_wait(0)
    relay(0)
    own_send(2)

    spread_wait(0, aux)
    fwd_first = [aux[q, :, 0:1] < 0.5 for q in range(YN)]
    bwd_first = [aux[q, :, 2:3] < 0.5 for q in range(YN)]

    def divide(block, first, target):
        zero = jnp.zeros_like(block)
        target[:, pl.ds(0, full)] = jnp.where(first, block, zero)
        target[:, pl.ds(full, full)] = jnp.where(first, zero, block)

    spread_wait(1, xf)
    for q in range(YN):
        divide(xf[q], fwd_first[q], xcat.at[q // 2, 0, q % 2])
    spread_wait(2, xb)
    for q in range(YN):
        divide(xb[q], bwd_first[q], xcat.at[q // 2, 1, q % 2])

    def gather_buffer(i):
        return hid[i] if i < ng else grads[i - ng]

    def gather_args(i, part, n, device):
        ref = gather_buffer(i).at[part]
        return ref, ref, ag_send.at[i, n], ag_recv.at[i, n], device

    def gather_send(i):
        targets = [across, my_outer] + ([far_outer] if i == items - 1 else [])
        for n, device in enumerate(targets):
            sent_by(inner_ending, functools.partial(gather_args, i, half, n, device))

    def gather_relay(i):
        @pl.when(inner)
        def _():
            arrive(gather_buffer(i).at[rest], ag_recv.at[i, 0])
            if i < items - 1:
                sent_by(inner_ending, functools.partial(gather_args, i, rest, 2, my_outer))

    def gather_wait(i):
        buffer = gather_buffer(i)

        @pl.when(outer)
        def _():
            arrive(buffer.at[half], ag_recv.at[i, 1])
            arrive(buffer.at[rest], ag_recv.at[i, 2])

    def stage_refs(i):
        if i < ng:
            return s1_out[i], s1_in[i], s2_out[i], s2_in[i], kept[i]
        d = i - ng
        return s1d_out[d], s1d_in[d], s2d_out[d], s2d_in[d], keptd[d]

    def near_args(i, n):
        out, into, _, _, _ = stage_refs(i)
        return out.at[n], into.at[n], s_send.at[i, n], s_recv.at[i, n], my_inner

    def across_args(i):
        _, _, out, across_in, _ = stage_refs(i)
        return out, across_in, s_send.at[i, 2], s_recv.at[i, 2], across

    def first_stage(i):
        if i < ng:
            mats = gu[i][...].reshape(XN * width, 2 * gates[i].size)
            source, count = xcat, 4
        else:
            mats = dn[i - ng][...].reshape(XN * width, downs[i - ng].size)
            source, count = gcat, 2
        out, into, _, _, keep = stage_refs(i)
        for n, owner in enumerate((rest, half)):
            rows = source.at[owner][...].reshape(count * tokens, 2 * full)
            partial_sum = jnp.dot(rows, mats, preferred_element_type=jnp.float32)
            keep[n] = partial_sum.reshape(keep.shape[1:])

            @pl.when(outer)
            def _():
                out[n] = keep[n].astype(jnp.bfloat16)
                sent_by(outer_ending, functools.partial(near_args, i, n))

    def second_stage(i):
        _, into, out, across_in, keep = stage_refs(i)

        @pl.when(inner)
        def _():
            arrive(into.at[0], s_recv.at[i, 0])
            out[...] = (keep[0] + into[0].astype(jnp.float32)).astype(jnp.bfloat16)
            sent_by(inner_ending, functools.partial(across_args, i))

    def third_stage(i):
        _, into, _, across_in, keep = stage_refs(i)

        @pl.when(inner)
        def _():
            arrive(into.at[1], s_recv.at[i, 1])
            arrive(across_in, s_recv.at[i, 2])
            if i < ng:
                c = gates[i].size
                sums = [
                    keep[1, b] + into[1, b].astype(jnp.float32) + across_in[b].astype(jnp.float32)
                    for b in range(2)
                ]
                back[i][...] = sums[1]
                gate, up = sums[0][:, :c], sums[0][:, c:]
                hid[i][half] = (gate * jax.nn.sigmoid(gate) * up).astype(jnp.bfloat16)
            else:
                d = i - ng
                c, home = downs[d].size, downs[d].parent
                at = downs[d].start - gates[home].start
                grad_hidden = (
                    keep[1] + into[1].astype(jnp.float32) + across_in[...].astype(jnp.float32)
                )
                gate = back[home][:, at : at + c]
                up = back[home][:, gates[home].size + at : gates[home].size + at + c]
                sig = jax.nn.sigmoid(gate)
                grad_gate = grad_hidden * up * sig * (1.0 + gate * (1.0 - sig))
                grad_up = grad_hidden * (gate * sig)
                grads[d][half, :, pl.ds(0, c)] = grad_gate.astype(jnp.bfloat16)
                grads[d][half, :, pl.ds(c, c)] = grad_up.astype(jnp.bfloat16)
            gather_send(i)

    def accumulate(values, first, mats, acc, start):
        zero = jnp.zeros_like(values[0])
        zeroth = jnp.concatenate([jnp.where(m, v, zero) for m, v in zip(first, values)], axis=0)
        other = jnp.concatenate([jnp.where(m, zero, v) for m, v in zip(first, values)], axis=0)
        total = lax.dot_general(zeroth, mats[:full], NT, preferred_element_type=jnp.float32)
        total += lax.dot_general(other, mats[full:], NT, preferred_element_type=jnp.float32)
        if start:
            acc[...] = total
        else:
            acc[...] += total

    def rows_of(buffer, at, c):
        return [
            buffer[q // 2, q % 2 * tokens : (q % 2 + 1) * tokens, at : at + c] for q in range(YN)
        ]

    def forward_sum(d):
        c, home = downs[d].size, downs[d].parent
        at = downs[d].start - gates[home].start
        if at == 0:
            gather_wait(home)
        mats = dn[d][...].reshape(XN * width, c)
        values = rows_of(hid[home], at, c)
        accumulate(values, fwd_first, mats, out_acc, d == 0)

    def backward_sum(d):
        c, home = downs[d].size, downs[d].parent
        at, size = downs[d].start - gates[home].start, gates[home].size
        gather_wait(ng + d)
        mats = gu[home][...].reshape(XN * width, 2 * size)
        if c != size:
            mats = jnp.concatenate([mats[:, at : at + c], mats[:, size + at : size + at + c]], axis=1)
        accumulate(rows_of(grads[d], 0, 2 * c), bwd_first, mats, grad_acc, d == 0)

    pieces = 2
    span = tokens // pieces

    def finished(number, q, residual, acc, where_lane):
        produced = acc[pl.ds(q * tokens, tokens), :].astype(jnp.bfloat16).astype(jnp.float32)
        weight = aux[q, :, where_lane : where_lane + 1]
        return (residual[q].astype(jnp.float32) + weight * produced).astype(jnp.bfloat16)

    def give(number, residual, acc, where_lane):
        for q in range(YN):
            ret_out[number, q] = finished(number, q, residual, acc, where_lane)

    def give_send(number, piece):
        rows = pl.ds(piece * span, span)
        for k in (2, 1, 3):
            other = (y + k) % YN
            sent(
                ret_out.at[number, other, rows],
                ret_in.at[number, y, rows],
                ret_send.at[number, piece, k],
                ret_recv.at[number, piece, k],
                column(k),
            )

    def give_own(number):
        ret_in[number, y] = ret_out[number, place]

    stores = []

    def collect(number, result):
        for piece in range(pieces):
            rows = pl.ds(piece * span, span)
            for k in range(1, YN):
                other = (y + YN - k) % YN
                arrive(ret_in.at[number, other, rows], ret_recv.at[number, piece, k])
        whole[number] = jnp.concatenate(
            [ret_in[number, t, :, h * width : (h + 1) * width] for h in range(2) for t in range(YN)],
            axis=1,
        )
        stores.append(pltpu.make_async_copy(whole.at[number], result, store.at[number]))
        stores[-1].start()

    for i in range(items):
        d = i - ng
        if i + 1 < items:
            direct_wait(i + 1)
            relay(i + 1)
            own_send(i + 3)
        relay_wait(i)
        for number, copy in locals_:
            if number == i:
                copy.wait()
        if i == ng:
            spread_wait(3, xg)
            for q in range(YN):
                divide(xg[q], bwd_first[q], gcat.at[q // 2, q % 2])
        first_stage(i)
        if i > 0:
            third_stage(i - 1)
        if d >= 1:
            forward_sum(d - 1)
        if d == nd - 1:
            forward_sum(d)
            give(0, xf, out_acc, 1)
        second_stage(i)
        if i > 0:
            gather_relay(i - 1)
        if i == items - 1:
            give_send(0, 0)
            give_own(0)
        if d >= 2:
            backward_sum(d - 2)

    if nd >= 2:
        backward_sum(nd - 2)
    third_stage(items - 1)
    give_send(0, 1)
    gather_relay(items - 1)
    backward_sum(nd - 1)
    give(1, xg, grad_acc, 3)
    give_send(1, 0)
    give_send(1, 1)
    give_own(1)
    collect(0, fwd_out)
    fwd_finish()
    grad_finish()
    for copy in ending:
        copy.wait_send()

    @pl.when(inner)
    def _():
        for args in inner_ending:
            remote(*args()).wait_send()

    @pl.when(outer)
    def _():
        for args in outer_ending:
            remote(*args()).wait_send()

    collect(1, bwd_out)
    for copy in stores:
        copy.wait()


def fused(arrays, sections):
    tokens, model = arrays[0].shape
    width, units = arrays[3].shape
    gates, downs = chunks_of(units)
    full = model // YN
    bf16, f32 = jnp.bfloat16, jnp.float32
    dma = pltpu.SemaphoreType.DMA
    items = len(gates) + len(downs)
    whole = jax.ShapeDtypeStruct((tokens, model), bf16)
    ups = [2 * c.size for c in gates]
    sizes = [c.size for c in downs]

    def each(lead, tail, counts, kind):
        return [pltpu.VMEM(lead + (n,) + tail, kind) for n in counts]

    scratch = []
    scratch += each((XN, width), (), ups, bf16)
    scratch += each((2, 2, 2 * tokens), (), ups, bf16)
    scratch += each((2, 2, 2 * tokens), (), ups, bf16)
    scratch += each((2, 2 * tokens), (), ups, bf16)
    scratch += each((2, 2 * tokens), (), ups, bf16)
    scratch += each((2, 2, 2 * tokens), (), ups, f32)
    scratch += each((2, 2 * tokens), (), [n // 2 for n in ups], bf16)
    scratch += each((2 * tokens,), (), ups, f32)
    scratch += each((XN, width), (), sizes, bf16)
    scratch += each((2, 2 * tokens), (), sizes, bf16)
    scratch += each((2, 2 * tokens), (), sizes, bf16)
    scratch += each((2 * tokens,), (), sizes, bf16)
    scratch += each((2 * tokens,), (), sizes, bf16)
    scratch += each((2, 2 * tokens), (), sizes, f32)
    scratch += each((2, 2 * tokens), (), [2 * n for n in sizes], bf16)
    scratch += [
        pltpu.VMEM((3, tokens, model), bf16),
        pltpu.VMEM((2, 1, tokens), jnp.int32),
        pltpu.VMEM((2, 1, tokens), f32),
        pltpu.VMEM((3, YN, tokens, full), bf16),
        pltpu.VMEM((tokens, 128), f32),
        pltpu.VMEM((YN, tokens, 128), f32),
        pltpu.VMEM((3, YN, tokens, full), bf16),
        pltpu.VMEM((2, 2, 2, tokens, 2 * full), bf16),
        pltpu.VMEM((2, 2, tokens, 2 * full), bf16),
        pltpu.VMEM((YN * tokens, full), f32),
        pltpu.VMEM((YN * tokens, full), f32),
        pltpu.VMEM((2, YN, tokens, full), bf16),
        pltpu.VMEM((2, YN, tokens, full), bf16),
        dma((7,)),
        dma((items, 2, 2)),
        dma((items, 2, 2)),
        dma((items, 2)),
        dma((items, 2)),
        dma((items, 2)),
        dma((4, 2 * YN)),
        dma((4, YN)),
        dma((items, 3)),
        dma((items, 3)),
        dma((items, YN - 1)),
        dma((items, YN - 1)),
        dma((2, 2, YN)),
        dma((2, 2, YN)),
        dma((2,)),
    ]
    return pl.pallas_call(
        functools.partial(kernel, sections, gates, downs),
        out_shape=(whole, whole),
        in_specs=[pl.BlockSpec(memory_space=pl.ANY)] * 10,
        out_specs=(pl.BlockSpec(memory_space=pl.ANY),) * 2,
        scratch_shapes=scratch,
        compiler_params=pltpu.CompilerParams(
            collective_id=0, has_side_effects=True, vmem_limit_bytes=62 * 1024 * 1024
        ),
    )(*arrays)


def body(sections, fwd_in, bwd_in, bwd_grad_in, w_gate, w_up, w_down, fwd_ids, fwd_gates, bwd_ids, bwd_gates):
    def line(values):
        return values.reshape(1, -1)

    arrays = [fwd_in[0], bwd_in[0], bwd_grad_in[0], w_gate[0], w_up[0], w_down[0].T]
    arrays += [line(fwd_ids), line(fwd_gates), line(bwd_ids), line(bwd_gates)]
    fwd, bwd = fused(arrays, sections)
    return fwd[None], bwd[None]


def solution(mesh):
    rows = P("pipe", "expert", None)
    return jax.shard_map(
        functools.partial(body, mesh.shape["pipe"]),
        mesh=mesh,
        in_specs=(rows, rows, rows, rows, rows, P("pipe", None, "expert"), rows, rows, rows, rows),
        out_specs=(rows, rows),
        check_vma=False,
    )
```
